256 devices in a mesh: basin: 64 (over z, x, core), ens: 4 (over y).
Axes of the slice: x: 4, y: 4, z: 8, core: 2. Of those that a mesh axis runs over, the one named last changes fastest.
Arguments:
- downstream: int32 [65536], P('basin'), may hold values from 0 to 65535, as said below
- bed_level: float32 [65536], P('basin'), may hold values from 0 to 3
- reach_length: float32 [65536], P('basin'), may hold values from 1000 to 5000
- channel_width: float32 [65536], P('basin'), may hold values from 50 to 300
- roughness: float32 [65536], P('basin'), may hold values from 0.025 to 0.06
- depth: float32 [65536, 512], P('basin', 'ens'), may hold values from 0.5 to 3
- flow: float32 [65536, 512], P('basin', 'ens'), may hold values from 0 to 2
- runoff: float32 [65536, 512], P('basin', 'ens'), may hold values from 0.0002 to 0.005
Outputs:
- new_depth: float32 [65536, 512], P('basin', 'ens')
- new_flow: float32 [65536, 512], P('basin', 'ens')
- mean_flow: float32 [65536], P('basin')
The draws below stay inside these ranges and needn't reach their ends.
Inputs may be any that keep to these rules, and one draw needn't show every extreme that they name: `downstream`: within the 1024 cells of one block, a cell drains either into a later cell of the same block, into itself (mouth), or into a cell of the next block or of the block after it along basin (main-stem segments); from one block at most 256 cells drain into each of these two, and exactly 256 into the next one wherever it exists.
All inputs are finite; a program needn't handle non-finite values.
Results may differ from the reference program's by a relative error of at most 0.0001.
Values sent between devices are 32-bit elements; how exact they have to be, the bound alone decides.
No kernel may reach another device: no remote copies, remote signals or barrier semaphores. Data moves between devices by JAX's collectives and lax.ppermute only.
A program may use at most 64 MiB of HBM per device.

```python
import math
import jax
import jax.numpy as jnp

CELL_DEV = 1024
ENS = 512
SLOTS = 256
STEPS = 4
CELLS = 65536
N_BASIN = 64


def draw_downstream(key, part):
    count = CELL_DEV
    inner = count - 2 * SLOTS
    device = jnp.arange(N_BASIN, dtype=jnp.int32)[:, None]
    place = jnp.arange(count, dtype=jnp.int32)[None, :]
    first_key = jax.random.fold_in(key, 11)
    second_key = jax.random.fold_in(key, 12)
    third_key = jax.random.fold_in(key, 13)
    order_key = jax.random.fold_in(key, 14)
    block_keys = jax.random.split(order_key, N_BASIN)
    rank = jax.vmap(lambda one: jax.random.permutation(one, count))(block_keys).astype(jnp.int32)
    spread_bits = jax.random.randint(first_key, (N_BASIN, count), 0, 2 ** 30)
    room = jnp.maximum(count - 1 - place, 1)
    local_down = place + 1 + spread_bits % room
    local_down = jnp.where(place == count - 1, place, local_down)
    group = (rank - inner) // SLOTS
    target_device = device + 1 + group
    target_cell = jax.random.randint(second_key, (N_BASIN, count), 0, count)
    live = (jax.random.randint(third_key, (N_BASIN, count), 0, 10) < 7) | (group == 0)
    live = live & (target_device < N_BASIN)
    remote_down = jnp.where(live, target_device * count + target_cell, device * count + place)
    result = jnp.where(rank < inner, device * count + local_down, remote_down)
    return result.reshape(-1).astype(jnp.int32)


def level_of(rng, dims, pieces, low, top_value):
    def one(axis_at, blocks):
        heights = jax.random.uniform(jax.random.fold_in(jax.random.fold_in(rng, 6), axis_at), (blocks,), jnp.float32, low / len(pieces), top_value / len(pieces))
        return jnp.repeat(jnp.exp(heights), dims[axis_at] // blocks).reshape((-1,) + (1,) * (len(dims) - axis_at - 1))

    factor_of = one(*pieces[0])
    for cut in pieces[1:]:
        factor_of = factor_of * one(*cut)
    return factor_of


def setup_inputs(seed: int = 0) -> dict:
    arg_keys = jax.random.split(jax.random.key(seed), 9)
    downstream = draw_downstream(jax.random.fold_in(arg_keys[8], 71), 0)
    bed_level = jnp.clip(3.0 * jax.random.uniform(arg_keys[1], (CELLS,), jnp.float32) ** level_of(arg_keys[1], (CELLS,), ((0, 64),), -0.2, 0.2), 0.0, 3.0)
    reach_length = jnp.clip(jnp.exp(math.log(5000.0) - 1.609438 * jax.random.uniform(arg_keys[2], (CELLS,), jnp.float32) ** level_of(arg_keys[2], (CELLS,), ((0, 64),), -0.2, 0.2)), 1000.0, 5000.0)
    channel_width = jnp.clip(jnp.exp(math.log(300.0) - 1.7917595 * jax.random.uniform(arg_keys[3], (CELLS,), jnp.float32) ** level_of(arg_keys[3], (CELLS,), ((0, 64),), -0.2, 0.2)), 50.0, 300.0)
    roughness = jnp.clip(jnp.exp(math.log(0.06) - 0.8754687 * jax.random.uniform(arg_keys[4], (CELLS,), jnp.float32) ** level_of(arg_keys[4], (CELLS,), ((0, 64),), -0.2, 0.2)), 0.025, 0.06)
    depth = jnp.clip(0.5 + 2.5 * jax.random.uniform(arg_keys[5], (CELLS, ENS), jnp.float32) ** level_of(arg_keys[5], (CELLS, ENS), ((0, 64), (1, 4)), -0.2, 0.2), 0.5, 3.0)
    flow = jnp.clip(2.0 * jax.random.uniform(arg_keys[6], (CELLS, ENS), jnp.float32) ** level_of(arg_keys[6], (CELLS, ENS), ((0, 64), (1, 4)), -0.2, 0.2), 0.0, 2.0)
    runoff = jnp.clip(jnp.exp(math.log(0.005) - 3.218876 * jax.random.uniform(arg_keys[7], (CELLS, ENS), jnp.float32) ** level_of(arg_keys[7], (CELLS, ENS), ((0, 64), (1, 4)), -0.2, 0.2)), 0.0002, 0.005)
    return dict(downstream=downstream, bed_level=bed_level, reach_length=reach_length, channel_width=channel_width, roughness=roughness, depth=depth, flow=flow, runoff=runoff)


GRAVITY = 9.81
TIME_STEP = 30.0
DEPTH_FLOOR = 0.25


def momentum(flow, depth, bed, level_down, bed_down, length, rough):
    level = bed + depth
    flow_depth = jnp.maximum(jnp.maximum(level, level_down) - jnp.maximum(bed, bed_down), DEPTH_FLOOR)
    slope = (level_down - level) / length
    friction = 1.0 + GRAVITY * TIME_STEP * rough * rough * jnp.abs(flow) / flow_depth ** (7.0 / 3.0)
    moved = (flow - GRAVITY * TIME_STEP * flow_depth * slope) / friction
    return jnp.minimum(moved, depth * length / (2.0 * TIME_STEP))


def reference(downstream, bed_level, reach_length, channel_width, roughness, depth, flow, runoff):
    count = downstream.shape[0]
    own = jnp.arange(count, dtype=jnp.int32)
    mouth = downstream == own
    bed_down = jnp.where(mouth, bed_level - 1.0, bed_level[downstream])
    area = (channel_width * reach_length)[:, None]
    for step in range(STEPS):
        level = bed_level[:, None] + depth
        level_down = jnp.where(mouth[:, None], bed_down[:, None], level[downstream])
        flow = momentum(flow, depth, bed_level[:, None], level_down, bed_down[:, None], reach_length[:, None], roughness[:, None])
        discharge = flow * channel_width[:, None]
        arriving = jax.ops.segment_sum(jnp.where(mouth[:, None], jnp.zeros_like(discharge), discharge), downstream, num_segments=count)
        depth = depth + TIME_STEP * (runoff + (arriving - discharge) / area)
    return depth, flow, jnp.sum(flow, axis=1) / ENS
```

```python
import functools

import jax
import jax.numpy as jnp
from jax import lax
from jax.experimental import pallas as pl
from jax.experimental.pallas import tpu as pltpu
from jax.sharding import PartitionSpec as P

SLOTS = 256
STEPS = 4
GRAVITY = 9.81
TIME_STEP = 30.0
DEPTH_FLOOR = 0.25
INTERPRET = False
F32 = jnp.float32
BF16 = jnp.bfloat16
N = 1024
L = 128
B = 256
NB = N // B
RB = 64


def split3(x):
    a = x.astype(BF16)
    r = x - a.astype(F32)
    b = r.astype(BF16)
    c = (r - b.astype(F32)).astype(BF16)
    return a, b, c


def put_split(ref, rows, x):
    a, b, c = split3(x)
    ref[rows, 0:L] = a
    ref[rows, L : 2 * L] = b
    ref[rows, 2 * L : 3 * L] = c


def joined(y):
    return (y[:, 0:L] + y[:, L : 2 * L]) + y[:, 2 * L : 3 * L]


def dot(a, b):
    return jnp.dot(a, b, preferred_element_type=F32)


def momentum(q, h, up, down, top, c1, c2, c3):
    deep = jnp.maximum(jnp.maximum(up, down) - top, DEPTH_FLOOR)
    push = deep * (down - up) * c1
    drag = 1.0 + c2 * jnp.abs(q) * jnp.exp((-7.0 / 3.0) * jnp.log(deep))
    return jnp.minimum((q - push) / drag, h * c3)


def as_row(x):
    return jnp.concatenate([x[k : k + 1, :] for k in range(8)], axis=1)


def onehot_cols(ref, rows, col, width, base=0):
    lane = lax.broadcasted_iota(jnp.int32, (col.shape[0], width), 1) + base
    ref[rows, 0:width] = jnp.where(lane == col, 1.0, 0.0).astype(BF16)


def flags(d):
    even = lax.rem(d, 2) == 0
    chip_even = lax.rem(lax.div(d, 2), 2) == 0
    return even, chip_even


def call(body, outs, scratch, flops, args, smem):
    spec_v = pl.BlockSpec(memory_space=pltpu.VMEM)
    spec_s = pl.BlockSpec(memory_space=pltpu.SMEM)
    return pl.pallas_call(
        body,
        out_shape=[jax.ShapeDtypeStruct(s, t) for s, t in outs],
        in_specs=[spec_s] * smem + [spec_v] * (len(args) - smem),
        out_specs=[spec_v] * len(outs),
        scratch_shapes=[pltpu.VMEM(s, t) for s, t in scratch],
        compiler_params=pltpu.CompilerParams(vmem_limit_bytes=32 * 1024 * 1024),
        cost_estimate=pl.CostEstimate(flops=flops, transcendentals=0, bytes_accessed=4 * 1024 * 1024),
        interpret=INTERPRET,
    )(*args)


def first_body(dev, down, bed, length, width, rough, flow, rows_out, cols_out, note1, note2, cmat, smat, fs):
    d = dev[0]
    even, chip_even = flags(d)
    place = lax.broadcasted_iota(jnp.int32, (8, L), 0) * L + lax.broadcasted_iota(jnp.int32, (8, L), 1)
    rel = down[...] - d * N
    hop = lax.shift_right_arithmetic(rel, 10)
    tri = (
        lax.broadcasted_iota(jnp.int32, (L, L), 0) <= lax.broadcasted_iota(jnp.int32, (L, L), 1)
    )
    tri = jnp.where(tri, 1.0, 0.0).astype(BF16)
    slots = []
    for k in (1, 2):
        mark = jnp.where(hop == k, 1.0, 0.0)
        lanes = dot(mark.astype(BF16), tri)
        totals = jnp.sum(mark, axis=1, keepdims=True)
        before = []
        running = jnp.zeros((1, 1), F32)
        for r in range(8):
            before.append(running)
            running = running + totals[r : r + 1, :]
        slots.append((lanes + jnp.concatenate(before, axis=0)).astype(jnp.int32) - 1)
    slot = jnp.where(hop == 1, slots[0], jnp.where(hop == 2, SLOTS + slots[1], -1))
    base1 = jnp.where(even, 0, SLOTS)
    base2 = jnp.where(chip_even, 2 * SLOTS, 3 * SLOTS)
    edge = jnp.where(hop == 1, slots[0] + base1, jnp.where(hop == 2, slots[1] + base2, -1))
    local = jnp.where((hop == 0) & (rel != place), rel, -1)
    mouth = jnp.where(rel == place, 1.0, 0.0)
    target = jnp.where(hop > 0, (rel & (N - 1)) + 1, 0)
    rows = jnp.concatenate(
        [
            as_row(local.astype(F32)),
            as_row(edge.astype(F32)),
            as_row(slot.astype(F32)),
            as_row(mouth),
            as_row(bed[...]),
            as_row(length[...]),
            as_row(width[...]),
            as_row(rough[...]),
        ],
        axis=0,
    )
    rows_out[...] = rows
    cols_out[:, 0:8] = rows.T
    sent = jnp.concatenate(
        [as_row(target.astype(F32)), rows[4:8, :], jnp.zeros((3, N), F32)], axis=0
    )
    a, b, c = split3(sent)
    stack = jnp.concatenate([a.astype(F32), b.astype(F32), c.astype(F32)], axis=0).astype(BF16)

    def build(k, carry):
        r = pl.ds(pl.multiple_of(k * RB, RB), RB)
        onehot_cols(cmat, r, cols_out[r, 2:3].astype(jnp.int32), 2 * SLOTS)
        put_split(fs, r, flow[r, :])
        return carry

    lax.fori_loop(0, N // RB, build, 0)

    def build_rows(k, carry):
        r = pl.ds(pl.multiple_of(k * RB, RB), RB)
        sub = lax.broadcasted_iota(jnp.int32, (RB, N), 0) + k * RB
        smat[r, :] = jnp.where(sub == rows_out[2:3, :].astype(jnp.int32), 1.0, 0.0).astype(BF16)
        return carry

    lax.fori_loop(0, 2 * SLOTS // RB, build_rows, 0)
    told = dot(stack, cmat[...])
    told = (told[0:8, :] + told[8:16, :]) + told[16:24, :]
    for k, note in enumerate((note1, note2)):
        note[0:SLOTS, :] = joined(dot(smat[k * SLOTS : (k + 1) * SLOTS, :], fs[...]))
        note[SLOTS : SLOTS + 8, :] = told[:, k * SLOTS : k * SLOTS + L]
        note[SLOTS + 8 : SLOTS + 16, :] = told[:, k * SLOTS + L : (k + 1) * SLOTS]


BED, BEDN, C1, C2, C3, WL, C4, REM = range(8)


def consts_body(rows, cols, depth, flow, runoff, mat, matt, keep, held, moved, hs, ds):
    def build(k, carry):
        r = pl.ds(pl.multiple_of(k * RB, RB), RB)
        onehot_cols(mat, r, cols[r, 0:1].astype(jnp.int32), N)
        sub = lax.broadcasted_iota(jnp.int32, (RB, N), 0) + k * RB
        matt[r, :] = jnp.where(sub == rows[0:1, :].astype(jnp.int32), 1.0, 0.0).astype(BF16)
        put_split(hs, r, depth[r, :])
        a, b, c = split3(jnp.broadcast_to(cols[r, 4:5], (RB, L)))
        lane = lax.broadcasted_iota(jnp.int32, (RB, L), 1)
        three = jnp.where(lane == 0, a.astype(F32), jnp.where(lane == 1, b.astype(F32), c.astype(F32)))
        hs[r, 3 * L : 4 * L] = three.astype(BF16)
        return carry

    lax.fori_loop(0, N // RB, build, 0)
    for k in range(NB):
        r = slice(k * B, (k + 1) * B)
        got = dot(mat[r, k * B : N], hs[k * B : N, :])
        below = (got[:, 3 * L : 3 * L + 1] + got[:, 3 * L + 1 : 3 * L + 2]) + got[:, 3 * L + 2 : 3 * L + 3]
        bed, length, width, rough = cols[r, 4:5], cols[r, 5:6], cols[r, 6:7], cols[r, 7:8]
        mouth = cols[r, 3:4]
        remote = jnp.where(cols[r, 1:2] >= 0.0, 1.0, 0.0)
        below = jnp.where(mouth > 0.0, bed - 1.0, below)
        keep[r, BED : BED + 1] = bed
        keep[r, BEDN : BEDN + 1] = below
        keep[r, C1 : C1 + 1] = (GRAVITY * TIME_STEP) / length
        keep[r, C2 : C2 + 1] = (GRAVITY * TIME_STEP) * rough * rough
        keep[r, C3 : C3 + 1] = length * (0.5 / TIME_STEP)
        keep[r, WL : WL + 1] = jnp.where(remote > 0.0, 0.0, width)
        keep[r, C4 : C4 + 1] = TIME_STEP / (width * length)
        keep[r, REM : REM + 1] = remote
        local_rows(r, joined(got), depth, flow, keep, moved, ds)
    local_rest(depth, runoff, matt, keep, moved, held, ds)


def local_rows(r, got, depth, flow, keep, moved, ds):
    h = depth[r, :]
    bed, below = keep[r, BED : BED + 1], keep[r, BEDN : BEDN + 1]
    q = momentum(
        flow[r, :],
        h,
        bed + h,
        below + got,
        jnp.maximum(bed, below),
        keep[r, C1 : C1 + 1],
        keep[r, C2 : C2 + 1],
        keep[r, C3 : C3 + 1],
    )
    moved[r, :] = q
    put_split(ds, r, q * keep[r, WL : WL + 1])


def local_rest(depth, runoff, matt, keep, moved, held, ds):
    for k in range(NB):
        r = slice(k * B, (k + 1) * B)
        got = joined(dot(matt[r, 0 : (k + 1) * B], ds[0 : (k + 1) * B, :]))
        net = got - moved[r, :] * keep[r, WL : WL + 1]
        held[r, :] = depth[r, :] + (TIME_STEP * runoff[r, :] + keep[r, C4 : C4 + 1] * net)


def local_body(depth, flow, runoff, mat, matt, keep, held, moved, hs, ds):
    def build(k, carry):
        r = pl.ds(pl.multiple_of(k * RB, RB), RB)
        put_split(hs, r, depth[r, :])
        return carry

    lax.fori_loop(0, N // RB, build, 0)
    for k in range(NB):
        r = slice(k * B, (k + 1) * B)
        got = joined(dot(mat[r, k * B : N], hs[k * B : N, :]))
        local_rows(r, got, depth, flow, keep, moved, ds)
    local_rest(depth, runoff, matt, keep, moved, held, ds)


EUP, EDN, E1, E2, E3, EW, EV = range(7)


def edges_body(
    dev, rows, cols, depth, note1, note2, got0, got1, got2, got3,
    emat, ematt, ekeep, eflow, out0, out1, out2, out3, hs, tmp, tmpt,
):
    d = dev[0]
    even, chip_even = flags(d)
    sends = (even, jnp.logical_not(even), chip_even, jnp.logical_not(chip_even))
    notes = (note1, note1, note2, note2)
    gots = (got0, got1, got2, got3)
    outs = (out0, out1, out2, out3)

    def build(k, carry):
        r = pl.ds(pl.multiple_of(k * RB, RB), RB)
        put_split(hs, r, depth[r, :])
        return carry

    lax.fori_loop(0, N // RB, build, 0)
    for k in range(4):
        mine = notes[k]
        other = gots[k]
        s = sends[k]
        e = slice(k * B, (k + 1) * B)
        eflow[e, :] = jnp.where(s, mine[0:B, :], other[0:B, :])
        left = jnp.where(s, mine[B : B + 8, :], other[B : B + 8, :])
        right = jnp.where(s, mine[B + 8 : B + 16, :], other[B + 8 : B + 16, :])
        said = jnp.concatenate([left, right], axis=1)
        saidt = said.T
        want = saidt[:, 0:1]
        ok = want > 0.0
        length = jnp.where(ok, saidt[:, 2:3], 1.0)
        width = saidt[:, 3:4]
        rough = saidt[:, 4:5]
        ekeep[e, EUP : EUP + 1] = saidt[:, 1:2]
        ekeep[e, E1 : E1 + 1] = (GRAVITY * TIME_STEP) / length
        ekeep[e, E2 : E2 + 1] = (GRAVITY * TIME_STEP) * rough * rough
        ekeep[e, E3 : E3 + 1] = length * (0.5 / TIME_STEP)
        ekeep[e, EW : EW + 1] = jnp.where(s, -width, width)
        ekeep[e, EV : EV + 1] = jnp.where(s, 1.0, 0.0) + jnp.zeros_like(width)
        tmp[:, 0:1] = want.astype(jnp.int32) - 1
        tmpt[...] = said.astype(jnp.int32)

        @pl.when(s)
        def _():
            def rows_of(j, carry):
                r = pl.ds(pl.multiple_of(k * B + j * RB, RB), RB)
                sub = lax.broadcasted_iota(jnp.int32, (RB, N), 0) + (k * B + j * RB)
                emat[r, :] = jnp.where(sub == rows[1:2, :].astype(jnp.int32), 1.0, 0.0).astype(BF16)
                return carry

            lax.fori_loop(0, B // RB, rows_of, 0)

            def cols_of(j, carry):
                r = pl.ds(pl.multiple_of(j * RB, RB), RB)
                lane = lax.broadcasted_iota(jnp.int32, (RB, B), 1) + k * B
                ematt[r, e] = jnp.where(lane == cols[r, 1:2].astype(jnp.int32), 1.0, 0.0).astype(BF16)
                return carry

            lax.fori_loop(0, N // RB, cols_of, 0)
            ekeep[e, EDN : EDN + 1] = jnp.zeros((B, 1), F32)

        @pl.when(jnp.logical_not(s))
        def _():
            def rows_of(j, carry):
                r = pl.ds(pl.multiple_of(k * B + j * RB, RB), RB)
                lane = lax.broadcasted_iota(jnp.int32, (RB, N), 1)
                hit = lane == tmp[pl.ds(pl.multiple_of(j * RB, RB), RB), 0:1]
                emat[r, :] = jnp.where(hit, 1.0, 0.0).astype(BF16)
                beds = jnp.where(hit, rows[4:5, :], 0.0)
                ekeep[r, EDN : EDN + 1] = jnp.sum(beds, axis=1, keepdims=True)
                return carry

            lax.fori_loop(0, B // RB, rows_of, 0)

            def cols_of(j, carry):
                r = pl.ds(pl.multiple_of(j * RB, RB), RB)
                sub = lax.broadcasted_iota(jnp.int32, (RB, B), 0) + (j * RB + 1)
                ematt[r, e] = jnp.where(sub == tmpt[0:1, :], 1.0, 0.0).astype(BF16)
                return carry

            lax.fori_loop(0, N // RB, cols_of, 0)

        outs[k][0:B, :] = joined(dot(emat[e, :], hs[...]))
        beds = jnp.broadcast_to(ekeep[e, EDN : EDN + 1], (B, L)).T
        outs[k][B : B + 8, :] = jnp.concatenate(
            [beds[0:1, 0:L], beds[0:1, L : 2 * L], jnp.zeros((6, L), F32)], axis=0
        )


def edge_flow(k, send, r, mine, other, ekeep, eflow):
    h1, h2 = mine[0:B, :], other[0:B, :]
    up = jnp.where(send, h1, h2)
    low = jnp.where(send, h2, h1)
    bed, below = ekeep[r, EUP : EUP + 1], ekeep[r, EDN : EDN + 1]
    return momentum(
        eflow[r, :],
        up,
        bed + up,
        below + low,
        jnp.maximum(bed, below),
        ekeep[r, E1 : E1 + 1],
        ekeep[r, E2 : E2 + 1],
        ekeep[r, E3 : E3 + 1],
    )


def main_body(first, last, dev, held, emat, ematt, ekeep_in, eflow, keep, m0, m1, m2, m3, g0, g1, g2, g3, *rest):
    d = dev[0]
    even, chip_even = flags(d)
    sends = (even, jnp.logical_not(even), chip_even, jnp.logical_not(chip_even))
    mine = (m0, m1, m2, m3)
    gots = (g0, g1, g2, g3)
    rest = list(rest)
    if last:
        moved, depth, out_flow, sums, es = rest
    else:
        depth, next_flow = rest[0:2]
        outs = rest[2:6]
        rest = rest[6:]
        if first:
            ekeep = rest.pop(0)
            ekeep[...] = ekeep_in[...]
        es, hs = rest
    if not first:
        ekeep = ekeep_in
    for k in range(4):
        r = slice(k * B, (k + 1) * B)
        if first:
            spread = jnp.concatenate(
                [
                    jnp.broadcast_to(gots[k][B : B + 1, :], (8, L)),
                    jnp.broadcast_to(gots[k][B + 1 : B + 2, :], (8, L)),
                ],
                axis=1,
            ).T
            ekeep[r, EDN : EDN + 1] = jnp.where(sends[k], spread[:, 0:1], ekeep_in[r, EDN : EDN + 1])
        q = edge_flow(k, sends[k], r, mine[k], gots[k], ekeep, eflow)
        if not last:
            next_flow[r, :] = q
        put_split(es, r, q * ekeep[r, EW : EW + 1])
        if last:
            a, b, c = split3(q * ekeep[r, EV : EV + 1])
            es[r, 3 * L : 4 * L] = a
            es[r, 4 * L : 5 * L] = b
            es[r, 5 * L : 6 * L] = c
    for k in range(NB):
        r = slice(k * B, (k + 1) * B)
        got = dot(ematt[r, :], es[...])
        h = held[r, :] + keep[r, C4 : C4 + 1] * joined(got)
        depth[r, :] = h
        if last:
            q = jnp.where(keep[r, REM : REM + 1] > 0.0, joined(got[:, 3 * L : 6 * L]), moved[r, :])
            out_flow[r, :] = q
            total = jnp.broadcast_to(jnp.sum(q, axis=1, keepdims=True), (B, L)).T
            sums[2 * k : 2 * k + 1, :] = total[0:1, 0:L]
            sums[2 * k + 1 : 2 * k + 2, :] = total[0:1, L : 2 * L]
        else:
            put_split(hs, r, h)
    if not last:
        for k in range(4):
            r = slice(k * B, (k + 1) * B)
            outs[k][...] = joined(dot(emat[r, :], hs[...]))


def routes(n):
    on = [(i, i ^ 1) for i in range(n)]
    cross = [(i, (((i - 1) % n) ^ 1) + 1) for i in range(n)]
    cross = [(i, j % n) for i, j in cross]
    near = [(i, i ^ 2) for i in range(n)]
    far = [(i, ((((i - 2) % n) ^ 2) + 2) % n) for i in range(n)]
    return on, cross, near, far


def exchange(parts, n):
    on, cross, near, far = routes(n)
    g3 = lax.ppermute(parts[3], "basin", far)
    g1 = lax.ppermute(parts[1], "basin", cross)
    g2 = lax.ppermute(parts[2], "basin", near)
    g0 = lax.ppermute(parts[0], "basin", on)
    return g0, g1, g2, g3


def per_device(downstream, bed_level, reach_length, channel_width, roughness, depth, flow, runoff):
    n = lax.axis_size("basin")
    dev = lax.axis_index("basin").astype(jnp.int32).reshape(1)
    tiles = [x.reshape(8, L) for x in (downstream, bed_level, reach_length, channel_width, roughness)]
    rows, cols, note1, note2 = call(
        first_body,
        [((8, N), F32), ((N, 8), F32), ((SLOTS + 16, L), F32), ((SLOTS + 16, L), F32)],
        [((N, 2 * SLOTS), BF16), ((2 * SLOTS, N), BF16), ((N, 3 * L), BF16)],
        2 * N * 512 * 512,
        [dev, *tiles, flow],
        1,
    )
    got = exchange((note1, note1, note2, note2), n)
    wide = ((N, L), F32)
    mat, matt, keep, held, moved = call(
        consts_body,
        [((N, N), BF16), ((N, N), BF16), ((N, 8), F32), wide, wide],
        [((N, 4 * L), BF16), ((N, 3 * L), BF16)],
        4 * N * N * 512,
        [rows, cols, depth, flow, runoff],
        0,
    )
    outs = call(
        edges_body,
        [((N, N), BF16), ((N, N), BF16), ((N, 8), F32), wide] + [((B + 8, L), F32)] * 4,
        [((N, 3 * L), BF16), ((B, 8), jnp.int32), ((8, B), jnp.int32)],
        4 * N * N * 512,
        [dev, rows, cols, depth, note1, note2, *got],
        1,
    )
    emat, ematt, ekeep, eflow = outs[:4]
    sent = outs[4:]
    for step in range(STEPS):
        first, last = step == 0, step == STEPS - 1
        got = exchange(sent, n)
        if not first:
            held, moved = call(
                local_body,
                [wide, wide],
                [((N, 3 * L), BF16), ((N, 3 * L), BF16)],
                4 * N * N * 512,
                [depth, moved, runoff, mat, matt, keep],
                0,
            )
        args = [dev, held, emat, ematt, ekeep, eflow, keep, *sent, *got]
        if last:
            depth, out_flow, sums = call(
                functools.partial(main_body, first, last),
                [wide, wide, ((8, L), F32)],
                [((N, 6 * L), BF16)],
                4 * N * N * 512,
                args + [moved],
                1,
            )
        else:
            res = call(
                functools.partial(main_body, first, last),
                [wide, wide] + [((B, L), F32)] * 4 + ([((N, 8), F32)] if first else []),
                [((N, 3 * L), BF16), ((N, 3 * L), BF16)],
                4 * N * N * 512,
                args,
                1,
            )
            depth, eflow = res[:2]
            sent = res[2:6]
            if first:
                ekeep = res[6]
    m = lax.axis_size("ens")
    total = sums
    parts = [lax.ppermute(sums, "ens", [(i, i ^ k) for i in range(m)]) for k in range(1, m)]
    if m == 4:
        me = lax.axis_index("ens")
        total = (sums + parts[0]) + (parts[1] + parts[2])
    else:
        for p in parts:
            total = total + p
    return depth, out_flow, (total / (m * depth.shape[1])).reshape(N)


def solution(mesh):
    placed = (
        P("basin"),
        P("basin"),
        P("basin"),
        P("basin"),
        P("basin"),
        P("basin", "ens"),
        P("basin", "ens"),
        P("basin", "ens"),
    )
    return jax.shard_map(
        per_device,
        mesh=mesh,
        in_specs=placed,
        out_specs=(P("basin", "ens"), P("basin", "ens"), P("basin")),
        check_vma=False,
    )
```

```python
import functools

import jax
import jax.numpy as jnp
from jax import lax
from jax.experimental import pallas as pl
from jax.experimental.pallas import tpu as pltpu
from jax.sharding import PartitionSpec as P

SLOTS = 256
STEPS = 4
GRAVITY = 9.81
TIME_STEP = 30.0
DEPTH_FLOOR = 0.25
INTERPRET = False
F32 = jnp.float32
BF16 = jnp.bfloat16
N = 1024
L = 128
B = 256
H = 512
RB = 64


def split2(x):
    a = x.astype(BF16)
    return a, (x - a.astype(F32)).astype(BF16)


def split3(x):
    a = x.astype(BF16)
    r = x - a.astype(F32)
    b = r.astype(BF16)
    c = (r - b.astype(F32)).astype(BF16)
    return a, b, c


def put_split(ref, rows, x):
    a, b = split2(x)
    ref[rows, 0:L] = a
    ref[rows, L : 2 * L] = b


def joined(y):
    return y[:, 0:L] + y[:, L : 2 * L]


def dot(a, b):
    return jnp.dot(a, b, preferred_element_type=F32)


def momentum(q, h, up, down, top, c1, c2, c3):
    deep = jnp.maximum(jnp.maximum(up, down) - top, DEPTH_FLOOR)
    push = deep * (down - up) * c1
    drag = 1.0 + c2 * jnp.abs(q) * jnp.exp((-7.0 / 3.0) * jnp.log(deep))
    return jnp.minimum((q - push) / drag, h * c3)


def as_row(x):
    return jnp.concatenate([x[k : k + 1, :] for k in range(8)], axis=1)


def as_int(x):
    return x.astype(jnp.int32)


def ones_where(mask):
    return jnp.where(mask, 1.0, 0.0).astype(BF16)


def blocks(total, size, body):
    def step(k, carry):
        body(pl.ds(pl.multiple_of(k * size, size), size), k * size)
        return carry

    lax.fori_loop(0, total // size, step, 0)


def flags(d):
    even = lax.rem(d, 2) == 0
    chip_even = lax.rem(lax.div(d, 2), 2) == 0
    return even, chip_even


def call(body, outs, scratch, flops, args, spaces):
    spec = {
        "s": pl.BlockSpec(memory_space=pltpu.SMEM),
        "v": pl.BlockSpec(memory_space=pltpu.VMEM),
        "h": pl.BlockSpec(memory_space=pltpu.HBM),
    }
    return pl.pallas_call(
        body,
        out_shape=[jax.ShapeDtypeStruct(s, t) for s, t in outs],
        in_specs=[spec[c] for c in spaces],
        out_specs=[spec["v"]] * len(outs),
        scratch_shapes=scratch,
        compiler_params=pltpu.CompilerParams(vmem_limit_bytes=32 * 1024 * 1024),
        cost_estimate=pl.CostEstimate(flops=flops, transcendentals=0, bytes_accessed=4 * 1024 * 1024),
        interpret=INTERPRET,
    )(*args)


def first_body(dev, down, bed, length, width, rough, flow_in, rows_out, cols_out, note1, note2, cmat, smat, fs, small, whole, flow, sems):
    loads = [pltpu.make_async_copy(down, whole, sems.at[0])]
    for k, x in enumerate((bed, length, width, rough)):
        loads.append(pltpu.make_async_copy(x, small.at[k], sems.at[k + 1]))
    loads.append(pltpu.make_async_copy(flow_in, flow, sems.at[5]))
    for x in loads:
        x.start()
    d = dev[0]
    even, chip_even = flags(d)
    place = lax.broadcasted_iota(jnp.int32, (8, L), 0) * L + lax.broadcasted_iota(jnp.int32, (8, L), 1)
    tri = ones_where(
        lax.broadcasted_iota(jnp.int32, (L, L), 0) <= lax.broadcasted_iota(jnp.int32, (L, L), 1)
    )
    for x in loads[:5]:
        x.wait()
    rel = whole[...] - d * N
    hop = lax.shift_right_arithmetic(rel, 10)
    slots = []
    for k in (1, 2):
        mark = jnp.where(hop == k, 1.0, 0.0)
        lanes = dot(mark.astype(BF16), tri)
        totals = jnp.sum(mark, axis=1, keepdims=True)
        before = []
        running = jnp.zeros((1, 1), F32)
        for r in range(8):
            before.append(running)
            running = running + totals[r : r + 1, :]
        slots.append(as_int(lanes + jnp.concatenate(before, axis=0)) - 1)
    slot = jnp.where(hop == 1, slots[0], jnp.where(hop == 2, SLOTS + slots[1], -1))
    local = jnp.where((hop == 0) & (rel != place), rel, -1)
    mouth = jnp.where(rel == place, 1.0, 0.0)
    target = jnp.where(hop > 0, (rel & (N - 1)) + 1, 0)
    rows = jnp.concatenate(
        [
            as_row(local.astype(F32)),
            as_row(slot.astype(F32)),
            as_row(target.astype(F32)),
            as_row(mouth),
            as_row(small[0]),
            as_row(small[1]),
            as_row(small[2]),
            as_row(small[3]),
        ],
        axis=0,
    )
    rows_out[...] = rows
    cols_out[:, 0:8] = rows.T
    sent = jnp.concatenate([rows[2:3, :], rows[4:8, :], jnp.zeros((3, N), F32)], axis=0)
    a, b, c = split3(sent)
    stack = jnp.concatenate([a.astype(F32), b.astype(F32), c.astype(F32)], axis=0).astype(BF16)

    def build_cols(r, at):
        lane = lax.broadcasted_iota(jnp.int32, (RB, H), 1)
        cmat[r, :] = ones_where(lane == as_int(cols_out[r, 1:2]))

    blocks(N, RB, build_cols)

    def build_rows(r, at):
        sub = lax.broadcasted_iota(jnp.int32, (RB, N), 0) + at
        smat[r, :] = ones_where(sub == as_int(rows_out[1:2, :]))

    blocks(H, RB, build_rows)
    told = dot(stack, cmat[...])
    told = (told[0:8, :] + told[8:16, :]) + told[16:24, :]
    loads[5].wait()
    blocks(N, RB, lambda r, at: put_split(fs, r, flow[r, :]))
    picked = joined(dot(smat[...], fs[...]))
    for k, note in enumerate((note1, note2)):
        note[0:SLOTS, :] = picked[k * SLOTS : (k + 1) * SLOTS, :]
        note[SLOTS : SLOTS + 8, :] = told[:, k * SLOTS : k * SLOTS + L]
        note[SLOTS + 8 : SLOTS + 16, :] = told[:, k * SLOTS + L : (k + 1) * SLOTS]


BED, BEDN, C1, C2, C3, WL, C4, REM = range(8)
EUP, EDN, E1, E2, E3, EW = range(6)


def facts_of(note):
    return jnp.concatenate([note[B : B + 8, :], note[B + 8 : B + 16, :]], axis=1)


def put_edge_columns(ekeep, e, said, sign):
    cols = said.T
    length = jnp.where(cols[:, 0:1] > 0.0, cols[:, 2:3], 1.0)
    rough = cols[:, 4:5]
    ekeep[e, EUP : EUP + 1] = cols[:, 1:2]
    ekeep[e, EDN : EDN + 1] = jnp.zeros_like(length)
    ekeep[e, E1 : E1 + 1] = (GRAVITY * TIME_STEP) / length
    ekeep[e, E2 : E2 + 1] = (GRAVITY * TIME_STEP) * rough * rough
    ekeep[e, E3 : E3 + 1] = length * (0.5 / TIME_STEP)
    ekeep[e, EW : EW + 1] = sign * cols[:, 3:4]
    return cols


def leaving_body(rows, cols, note1, note2, depth_in, es, ets, ekeep, mine, hs, depth, sem):
    load = pltpu.make_async_copy(depth_in, depth, sem)
    load.start()
    for k, note in enumerate((note1, note2)):
        put_edge_columns(ekeep, slice(k * B, (k + 1) * B), facts_of(note), -1.0)

    def build_cols(r, at):
        lane = lax.broadcasted_iota(jnp.int32, (RB, H), 1)
        ets[r, :] = ones_where(lane == as_int(cols[r, 1:2]))

    blocks(N, RB, build_cols)

    def build_rows(r, at):
        sub = lax.broadcasted_iota(jnp.int32, (RB, N), 0) + at
        es[r, :] = ones_where(sub == as_int(rows[1:2, :]))

    blocks(H, RB, build_rows)
    load.wait()
    blocks(N, RB, lambda r, at: put_split(hs, r, depth[r, :]))
    mine[...] = joined(dot(es[...], hs[...]))


def route(even, chip_even, outs, s1, s2, r1, r2):
    outs[0][0:B, :] = jnp.where(even, s1, r1)
    outs[1][0:B, :] = jnp.where(even, r1, s1)
    outs[2][0:B, :] = jnp.where(chip_even, s2, r2)
    outs[3][0:B, :] = jnp.where(chip_even, r2, s2)


def entering_body(
    dev, rows, note1, note2, got0, got1, got2, got3, hs, mine_s, ekeep_s,
    er, etr, ekeep, eflow, mine, out0, out1, out2, out3, want,
):
    even, chip_even = flags(dev[0])
    outs = (out0, out1, out2, out3)
    ekeep[0:H, :] = ekeep_s[...]
    eflow[0:B, :] = note1[0:B, :]
    eflow[B:H, :] = note2[0:B, :]
    for k, (flag, a, b) in enumerate(((even, got1, got0), (chip_even, got3, got2))):
        e = slice(H + k * B, H + (k + 1) * B)
        eflow[e, :] = jnp.where(flag, a[0:B, :], b[0:B, :])
        said = jnp.where(flag, facts_of(a), facts_of(b))
        cols = put_edge_columns(ekeep, e, said, 1.0)
        here = slice(k * B, (k + 1) * B)
        want[here, 0:1] = as_int(cols[:, 0:1]) - 1
        wanted = as_int(said[0:1, :]) - 1

        def build_cols(r, at):
            sub = lax.broadcasted_iota(jnp.int32, (RB, B), 0) + at
            etr[r, here] = ones_where(sub == wanted)

        blocks(N, RB, build_cols)

    def build_rows(r, at):
        hit = lax.broadcasted_iota(jnp.int32, (RB, N), 1) == want[r, 0:1]
        er[r, :] = ones_where(hit)
        beds = jnp.sum(jnp.where(hit, rows[4:5, :], 0.0), axis=1, keepdims=True)
        ekeep[pl.ds(pl.multiple_of(at + H, RB), RB), EDN : EDN + 1] = beds

    blocks(H, RB, build_rows)
    mine[0:H, :] = mine_s[...]
    mine[H:N, :] = joined(dot(er[...], hs[...]))
    route(
        even, chip_even, outs,
        mine[0:B, :], mine[B:H, :], mine[H : H + B, :], mine[H + B : N, :],
    )
    tails = []
    for k in range(2):
        e = slice(H + k * B, H + (k + 1) * B)
        beds = jnp.broadcast_to(ekeep[e, EDN : EDN + 1], (B, L)).T
        tails.append(
            jnp.concatenate([beds[0:1, 0:L], beds[0:1, L : 2 * L], jnp.zeros((6, L), F32)], axis=0)
        )
    for k, out in enumerate(outs):
        out[B : B + 8, :] = tails[k // 2]


def local_part(depth, hs, flow, runoff, mat, matt, keep, held, moved, ds):
    for a, b in ((0, H), (H, N)):
        r = slice(a, b)
        got = joined(dot(mat[r, a:N], hs[a:N, :]))
        h = depth[r, :]
        bed, below = keep[r, BED : BED + 1], keep[r, BEDN : BEDN + 1]
        q = momentum(
            flow[r, :],
            h,
            bed + h,
            below + got,
            jnp.maximum(bed, below),
            keep[r, C1 : C1 + 1],
            keep[r, C2 : C2 + 1],
            keep[r, C3 : C3 + 1],
        )
        moved[r, :] = q
        put_split(ds, r, q * keep[r, WL : WL + 1])
    for a, b in ((0, H), (H, N)):
        r = slice(a, b)
        got = joined(dot(matt[r, 0:b], ds[0:b, :]))
        net = got - moved[r, :] * keep[r, WL : WL + 1]
        held[r, :] = depth[r, :] + (TIME_STEP * runoff[r, :] + keep[r, C4 : C4 + 1] * net)


def start_body(rows, cols, hs, depth_in, flow_in, runoff_in, mat, matt, keep, held, moved, runoff, depth, flow, ds, sems):
    loads = [
        pltpu.make_async_copy(a, b, sems.at[k])
        for k, (a, b) in enumerate(((depth_in, depth), (flow_in, flow), (runoff_in, runoff)))
    ]
    for x in loads:
        x.start()

    def build(r, at):
        hit = lax.broadcasted_iota(jnp.int32, (RB, N), 1) == as_int(cols[r, 0:1])
        mat[r, :] = ones_where(hit)
        keep[r, BEDN : BEDN + 1] = jnp.sum(jnp.where(hit, rows[4:5, :], 0.0), axis=1, keepdims=True)
        sub = lax.broadcasted_iota(jnp.int32, (RB, N), 0) + at
        matt[r, :] = ones_where(sub == as_int(rows[0:1, :]))

    blocks(N, RB, build)

    def columns(r, at):
        bed, length, width, rough = cols[r, 4:5], cols[r, 5:6], cols[r, 6:7], cols[r, 7:8]
        remote = cols[r, 1:2] >= 0.0
        keep[r, BED : BED + 1] = bed
        keep[r, BEDN : BEDN + 1] = jnp.where(cols[r, 3:4] > 0.0, bed - 1.0, keep[r, BEDN : BEDN + 1])
        keep[r, C1 : C1 + 1] = (GRAVITY * TIME_STEP) / length
        keep[r, C2 : C2 + 1] = (GRAVITY * TIME_STEP) * rough * rough
        keep[r, C3 : C3 + 1] = length * (0.5 / TIME_STEP)
        keep[r, WL : WL + 1] = jnp.where(remote, 0.0, width)
        keep[r, C4 : C4 + 1] = TIME_STEP / (width * length)
        keep[r, REM : REM + 1] = jnp.where(remote, 1.0, 0.0)

    blocks(N, RB, columns)
    for x in loads:
        x.wait()
    local_part(depth, hs, flow, runoff, mat, matt, keep, held, moved, ds)


def local_body(depth, hs, flow, runoff, mat, matt, keep, held, moved, ds):
    local_part(depth, hs, flow, runoff, mat, matt, keep, held, moved, ds)


def edges_now(first, flags2, ekeep, eflow, mine, gots, store):
    even, chip_even = flags2
    g0, g1, g2, g3 = gots
    if first:
        for k, (flag, a, b) in enumerate(((even, g0, g1), (chip_even, g2, g3))):
            told = jnp.where(flag, a[B : B + 8, :], b[B : B + 8, :])
            spread = jnp.concatenate(
                [jnp.broadcast_to(told[0:1, :], (8, L)), jnp.broadcast_to(told[1:2, :], (8, L))],
                axis=1,
            ).T
            ekeep[k * B : (k + 1) * B, EDN : EDN + 1] = spread[:, 0:1]
    choice = ((even, g0, g1), (chip_even, g2, g3), (even, g1, g0), (chip_even, g3, g2))
    for k, (flag, a, b) in enumerate(choice):

        def part(r, at):
            e = pl.ds(pl.multiple_of(at + k * B, L), L)
            theirs = jnp.where(flag, a[r, :], b[r, :])
            ours = mine[e, :]
            up, low = (ours, theirs) if k < 2 else (theirs, ours)
            bed, below = ekeep[e, EUP : EUP + 1], ekeep[e, EDN : EDN + 1]
            q = momentum(
                eflow[e, :],
                up,
                bed + up,
                below + low,
                jnp.maximum(bed, below),
                ekeep[e, E1 : E1 + 1],
                ekeep[e, E2 : E2 + 1],
                ekeep[e, E3 : E3 + 1],
            )
            store(k, e, q)

        blocks(B, L, part)


def main_body(first, dev, held, es, er, ets, etr, ekeep_in, eflow, keep, mine, g0, g1, g2, g3, depth, hs, next_flow, sent, o0, o1, o2, o3, *rest):
    even, chip_even = flags(dev[0])
    if first:
        ekeep, ds = rest
        ekeep[...] = ekeep_in[...]
    else:
        ekeep = ekeep_in
        (ds,) = rest

    def store(k, e, q):
        next_flow[e, :] = q
        put_split(ds, e, q * ekeep[e, EW : EW + 1])

    edges_now(first, (even, chip_even), ekeep, eflow, mine, (g0, g1, g2, g3), store)
    for a, b in ((0, H), (H, N)):
        r = slice(a, b)
        got = joined(dot(ets[r, :], ds[0:H, :]) + dot(etr[r, :], ds[H:N, :]))
        h = held[r, :] + keep[r, C4 : C4 + 1] * got
        depth[r, :] = h
        put_split(hs, r, h)
    sent[0:H, :] = joined(dot(es[...], hs[...]))
    sent[H:N, :] = joined(dot(er[...], hs[...]))
    route(
        even, chip_even, (o0, o1, o2, o3),
        sent[0:B, :], sent[B:H, :], sent[H : H + B, :], sent[H + B : N, :],
    )


def last_flow_body(dev, ets, ekeep, eflow, keep, moved, mine, g0, g1, g2, g3, ds, out_flow, sums, qs):
    def store(k, e, q):
        put_split(ds, e, q * ekeep[e, EW : EW + 1])
        if k < 2:
            put_split(qs, e, q)

    edges_now(False, flags(dev[0]), ekeep, eflow, mine, (g0, g1, g2, g3), store)
    for a, b in ((0, H), (H, N)):
        r = slice(a, b)
        got = joined(dot(ets[r, :], qs[...]))
        q = jnp.where(keep[r, REM : REM + 1] > 0.0, got, moved[r, :])
        out_flow[r, :] = q
        for k in range(a // L, b // L):
            part = q[k * L - a : (k + 1) * L - a, :].T
            sums[k : k + 1, :] = jnp.sum(part, axis=0, keepdims=True)


def last_depth_body(held, ets, etr, keep, ds, depth):
    for a, b in ((0, H), (H, N)):
        r = slice(a, b)
        got = joined(dot(ets[r, :], ds[0:H, :]) + dot(etr[r, :], ds[H:N, :]))
        depth[r, :] = held[r, :] + keep[r, C4 : C4 + 1] * got


def routes(n):
    on = [(i, i ^ 1) for i in range(n)]
    cross = [(i, (((i - 1) % n) ^ 1) + 1) for i in range(n)]
    cross = [(i, j % n) for i, j in cross]
    near = [(i, i ^ 2) for i in range(n)]
    far = [(i, ((((i - 2) % n) ^ 2) + 2) % n) for i in range(n)]
    return on, cross, near, far


def exchange(parts, n):
    on, cross, near, far = routes(n)
    g3 = lax.ppermute(parts[3], "basin", far)
    g1 = lax.ppermute(parts[1], "basin", cross)
    g2 = lax.ppermute(parts[2], "basin", near)
    g0 = lax.ppermute(parts[0], "basin", on)
    return g0, g1, g2, g3


def per_device(downstream, bed_level, reach_length, channel_width, roughness, depth, flow, runoff):
    n = lax.axis_size("basin")
    dev = lax.axis_index("basin").astype(jnp.int32).reshape(1)
    tiles = [x.reshape(8, L) for x in (downstream, bed_level, reach_length, channel_width, roughness)]
    wide, split = ((N, L), F32), ((N, 2 * L), BF16)
    narrow = ((N, 8), F32)
    note = ((SLOTS + 16, L), F32)
    vm = lambda st: pltpu.VMEM(*st)
    work = 4 * N * N * 512
    rows, cols, note1, note2 = call(
        first_body,
        [((8, N), F32), narrow, note, note],
        [
            pltpu.VMEM((N, H), BF16),
            pltpu.VMEM((H, N), BF16),
            vm(split),
            pltpu.VMEM((4, 8, L), F32),
            pltpu.VMEM((8, L), jnp.int32),
            vm(wide),
            pltpu.SemaphoreType.DMA((6,)),
        ],
        work,
        [dev, *tiles, flow],
        "shhhhhh",
    )
    got = exchange((note1, note1, note2, note2), n)
    es, ets, ekeep_s, mine_s, hs = call(
        leaving_body,
        [((H, N), BF16), ((N, H), BF16), ((H, 8), F32), ((H, L), F32), split],
        [vm(wide), pltpu.SemaphoreType.DMA],
        work,
        [rows, cols, note1, note2, depth],
        "vvvvh",
    )
    er, etr, ekeep, eflow, mine, *sent = call(
        entering_body,
        [((H, N), BF16), ((N, H), BF16), narrow, wide, wide] + [((B + 8, L), F32)] * 4,
        [pltpu.VMEM((H, 8), jnp.int32)],
        work,
        [dev, rows, note1, note2, *got, hs, mine_s, ekeep_s],
        "s" + "v" * 10,
    )
    for step in range(STEPS):
        got = exchange(sent, n)
        if step == 0:
            mat, matt, keep, held, moved, rain = call(
                start_body,
                [((N, N), BF16), ((N, N), BF16), narrow, wide, wide, wide],
                [vm(wide), vm(wide), vm(split), pltpu.SemaphoreType.DMA((3,))],
                work,
                [rows, cols, hs, depth, flow, runoff],
                "vvvhhh",
            )
        else:
            held, moved = call(
                local_body,
                [wide, wide],
                [vm(split)],
                work,
                [depth, hs, moved, rain, mat, matt, keep],
                "v" * 7,
            )
        if step == STEPS - 1:
            ds, out_flow, sums = call(
                last_flow_body,
                [split, wide, ((8, L), F32)],
                [pltpu.VMEM((H, 2 * L), BF16)],
                work,
                [dev, ets, ekeep, eflow, keep, moved, mine, *got],
                "s" + "v" * 10,
            )
        else:
            depth, hs, eflow, mine, *sent = call(
                functools.partial(main_body, step == 0),
                [wide, split, wide, wide] + [((B, L), F32)] * 4 + ([narrow] if step == 0 else []),
                [vm(split)],
                work,
                [dev, held, es, er, ets, etr, ekeep, eflow, keep, mine, *got],
                "s" + "v" * 13,
            )
            if step == 0:
                ekeep = sent.pop()
    m = lax.axis_size("ens")
    parts = [lax.ppermute(sums, "ens", [(i, i ^ k) for i in range(m)]) for k in range(1, m)]
    (depth,) = call(last_depth_body, [wide], [], work, [held, ets, etr, keep, ds], "v" * 5)
    if m == 4:
        total = (sums + parts[0]) + (parts[1] + parts[2])
    else:
        total = sums + parts[0]
    return depth, out_flow, (total / (m * depth.shape[1])).reshape(N)


def solution(mesh):
    placed = (
        P("basin"),
        P("basin"),
        P("basin"),
        P("basin"),
        P("basin"),
        P("basin", "ens"),
        P("basin", "ens"),
        P("basin", "ens"),
    )
    return jax.shard_map(
        per_device,
        mesh=mesh,
        in_specs=placed,
        out_specs=(P("basin", "ens"), P("basin", "ens"), P("basin")),
        check_vma=False,
    )
```

```python
import functools

import jax
import jax.numpy as jnp
from jax import lax
from jax.experimental import pallas as pl
from jax.experimental.pallas import tpu as pltpu
from jax.sharding import PartitionSpec as P

SLOTS = 256
STEPS = 4
GRAVITY = 9.81
TIME_STEP = 30.0
DEPTH_FLOOR = 0.25
INTERPRET = False
F32 = jnp.float32
BF16 = jnp.bfloat16
N = 1024
L = 128
B = 256
H = 512
RB = 64


def split2(x):
    a = x.astype(BF16)
    return a, (x - a.astype(F32)).astype(BF16)


def split3(x):
    a = x.astype(BF16)
    r = x - a.astype(F32)
    b = r.astype(BF16)
    c = (r - b.astype(F32)).astype(BF16)
    return a, b, c


def put_split(ref, rows, x):
    a, b = split2(x)
    ref[rows, 0:L] = a
    ref[rows, L : 2 * L] = b


def joined(y):
    return y[:, 0:L] + y[:, L : 2 * L]


def dot(a, b):
    return jnp.dot(a, b, preferred_element_type=F32)


def momentum(q, h, up, down, top, c1, c2, c3):
    deep = jnp.maximum(jnp.maximum(up, down) - top, DEPTH_FLOOR)
    push = deep * (down - up) * c1
    drag = 1.0 + c2 * jnp.abs(q) * jnp.exp((-7.0 / 3.0) * jnp.log(deep))
    return jnp.minimum((q - push) / drag, h * c3)


def as_row(x):
    return jnp.concatenate([x[k : k + 1, :] for k in range(8)], axis=1)


def as_int(x):
    return x.astype(jnp.int32)


def ones_where(mask):
    return jnp.where(mask, 1.0, 0.0).astype(BF16)


def blocks(total, size, body):
    def step(k, carry):
        body(pl.ds(pl.multiple_of(k * size, size), size), k * size)
        return carry

    lax.fori_loop(0, total // size, step, 0)


def flags(d):
    even = lax.rem(d, 2) == 0
    chip_even = lax.rem(lax.div(d, 2), 2) == 0
    return even, chip_even


def call(body, outs, scratch, flops, args, spaces):
    spec = {
        "s": pl.BlockSpec(memory_space=pltpu.SMEM),
        "v": pl.BlockSpec(memory_space=pltpu.VMEM),
        "h": pl.BlockSpec(memory_space=pltpu.HBM),
    }
    return pl.pallas_call(
        body,
        out_shape=[jax.ShapeDtypeStruct(s, t) for s, t in outs],
        in_specs=[spec[c] for c in spaces],
        out_specs=[spec["v"]] * len(outs),
        scratch_shapes=scratch,
        compiler_params=pltpu.CompilerParams(vmem_limit_bytes=32 * 1024 * 1024),
        cost_estimate=pl.CostEstimate(flops=flops, transcendentals=0, bytes_accessed=4 * 1024 * 1024),
        interpret=INTERPRET,
    )(*args)


def first_body(dev, facts, rows_out, cols_out, ets, note1, note2):
    d = dev[0]
    place = lax.broadcasted_iota(jnp.int32, (8, L), 0) * L + lax.broadcasted_iota(jnp.int32, (8, L), 1)
    tri = ones_where(
        lax.broadcasted_iota(jnp.int32, (L, L), 0) <= lax.broadcasted_iota(jnp.int32, (L, L), 1)
    )
    rel = as_int(facts[0]) - d * N
    hop = lax.shift_right_arithmetic(rel, 10)
    slots = []
    for k in (1, 2):
        mark = jnp.where(hop == k, 1.0, 0.0)
        lanes = dot(mark.astype(BF16), tri)
        totals = jnp.sum(mark, axis=1, keepdims=True)
        before = []
        running = jnp.zeros((1, 1), F32)
        for r in range(8):
            before.append(running)
            running = running + totals[r : r + 1, :]
        slots.append(as_int(lanes + jnp.concatenate(before, axis=0)) - 1)
    remote = hop > 0
    slot = jnp.where(hop == 1, slots[0], jnp.where(hop == 2, SLOTS + slots[1], -1))
    local = jnp.where((hop == 0) & (rel != place), rel, -1)
    target = jnp.where(remote, (rel & (N - 1)) + 1, 0)
    bed, length, width, rough = facts[1], facts[2], facts[3], facts[4]
    zero = jnp.zeros_like(bed)
    columns = [
        local.astype(F32),
        slot.astype(F32),
        target.astype(F32),
        bed,
        (GRAVITY * TIME_STEP) / length,
        (GRAVITY * TIME_STEP) * rough * rough,
        length * (0.5 / TIME_STEP),
        width,
        jnp.where(remote, 0.0, width),
        TIME_STEP / (width * length),
        jnp.where(remote, 1.0, 0.0),
        jnp.where(rel == place, bed - 1.0, 0.0),
        zero,
        zero,
        zero,
        zero,
    ]
    rows = jnp.concatenate([as_row(x) for x in columns], axis=0)
    rows_out[...] = rows
    cols_out[...] = rows.T
    sent = jnp.concatenate([rows[2:8, :], jnp.zeros((2, N), F32)], axis=0)
    a, b, c = split3(sent)
    stack = jnp.concatenate([a.astype(F32), b.astype(F32), c.astype(F32)], axis=0).astype(BF16)

    def build_cols(r, at):
        lane = lax.broadcasted_iota(jnp.int32, (B, H), 1)
        ets[r, :] = ones_where(lane == as_int(cols_out[r, SLOT : SLOT + 1]))

    blocks(N, B, build_cols)
    told = dot(stack, ets[...])
    told = (told[0:8, :] + told[8:16, :]) + told[16:24, :]
    for k, note in enumerate((note1, note2)):
        note[0:8, :] = told[:, k * SLOTS : k * SLOTS + L]
        note[8:16, :] = told[:, k * SLOTS + L : (k + 1) * SLOTS]


LOCAL, SLOT, TARGET, BED, C1, C2, C3, WIDTH, WL, C4, REM, SEA = range(12)
WANT, EUP, E1, E2, E3, EW, EDN = range(7)


def facts_of(note):
    return jnp.concatenate([note[0:8, :], note[8:16, :]], axis=1)


def leaving_body(rows, cols, depth, flow, es, mat, below, mine, first_flow, hs, fs):
    def build_rows(r, at):
        sub = lax.broadcasted_iota(jnp.int32, (RB, N), 0) + at
        es[r, :] = ones_where(sub == as_int(rows[SLOT : SLOT + 1, :]))

    blocks(H, RB, build_rows)

    def splits(r, at):
        put_split(hs, r, depth[r, :])
        put_split(fs, r, flow[r, :])

    blocks(N, L, splits)
    mine[...] = joined(dot(es[...], hs[...]))
    first_flow[...] = joined(dot(es[...], fs[...]))

    def build(r, at):
        hit = lax.broadcasted_iota(jnp.int32, (RB, N), 1) == as_int(cols[r, LOCAL : LOCAL + 1])
        mat[r, :] = ones_where(hit)
        beds = jnp.sum(jnp.where(hit, rows[BED : BED + 1, :], 0.0), axis=1, keepdims=True)
        below[r, 0:1] = beds + cols[r, SEA : SEA + 1]

    blocks(N, RB, build)


def route(even, chip_even, outs, s1, s2, r1, r2):
    outs[0][0:B, :] = jnp.where(even, s1, r1)
    outs[1][0:B, :] = jnp.where(even, r1, s1)
    outs[2][0:B, :] = jnp.where(chip_even, s2, r2)
    outs[3][0:B, :] = jnp.where(chip_even, r2, s2)


def entering_body(
    dev, rows, note1, note2, got0, got1, got2, got3, hs, mine_s, flow_s,
    er, etr, ekeep, mine, out0, out1, out2, out3,
):
    even, chip_even = flags(dev[0])
    outs = (out0, out1, out2, out3)
    for k, note in enumerate((note1, note2)):
        ekeep[k * B : (k + 1) * B, :] = facts_of(note).T
    wants = []
    for k, (flag, a, b) in enumerate(((even, got1, got0), (chip_even, got3, got2))):
        said = jnp.where(flag, facts_of(a), facts_of(b))
        ekeep[H + k * B : H + (k + 1) * B, :] = said.T
        wants.append(said[0:1, :])
    wanted = as_int(jnp.concatenate(wants, axis=1)) - 1

    def build_rows(r, at):
        e = pl.ds(pl.multiple_of(at + H, RB), RB)
        hit = lax.broadcasted_iota(jnp.int32, (RB, N), 1) == as_int(ekeep[e, WANT : WANT + 1]) - 1
        er[r, :] = ones_where(hit)
        beds = jnp.sum(jnp.where(hit, rows[BED : BED + 1, :], 0.0), axis=1, keepdims=True)
        ekeep[e, EDN : EDN + 1] = beds

    blocks(H, RB, build_rows)

    def build_cols(r, at):
        sub = lax.broadcasted_iota(jnp.int32, (L, H), 0) + at
        etr[r, :] = ones_where(sub == wanted)

    blocks(N, L, build_cols)
    mine[0:H, :] = mine_s[...]
    mine[H:N, :] = joined(dot(er[...], hs[...]))
    route(
        even, chip_even, outs,
        mine[0:B, :], mine[B:H, :], mine[H : H + B, :], mine[H + B : N, :],
    )
    for k in range(2):
        e = slice(H + k * B, H + (k + 1) * B)
        beds = jnp.broadcast_to(ekeep[e, EDN : EDN + 1], (B, L)).T
        tail = jnp.concatenate([beds[0:1, 0:L], beds[0:1, L : 2 * L], jnp.zeros((6, L), F32)], axis=0)
        for out in outs[2 * k : 2 * k + 2]:
            out[B:H, :] = flow_s[k * B : (k + 1) * B, :]
            out[H : H + 8, :] = tail


def local_part(depth, hs, flow, runoff, mat, matt, keep, below, held, moved, ds):
    for a, b in ((0, H), (H, N)):
        r = slice(a, b)
        got = joined(dot(mat[r, a:N], hs[a:N, :]))
        h = depth[r, :]
        bed, low = keep[r, BED : BED + 1], below[r, 0:1]
        q = momentum(
            flow[r, :],
            h,
            bed + h,
            low + got,
            jnp.maximum(bed, low),
            keep[r, C1 : C1 + 1],
            keep[r, C2 : C2 + 1],
            keep[r, C3 : C3 + 1],
        )
        moved[r, :] = q
        put_split(ds, r, q * keep[r, WL : WL + 1])
    for a, b in ((0, H), (H, N)):
        r = slice(a, b)
        got = joined(dot(matt[r, 0:b], ds[0:b, :]))
        net = got - moved[r, :] * keep[r, WL : WL + 1]
        held[r, :] = depth[r, :] + (TIME_STEP * runoff[r, :] + keep[r, C4 : C4 + 1] * net)


def start_body(rows, keep, depth, hs, flow, runoff, mat, below, matt, held, moved, ds):
    def build(r, at):
        sub = lax.broadcasted_iota(jnp.int32, (RB, N), 0) + at
        matt[r, :] = ones_where(sub == as_int(rows[LOCAL : LOCAL + 1, :]))

    blocks(N, RB, build)
    local_part(depth, hs, flow, runoff, mat, matt, keep, below, held, moved, ds)


def local_body(depth, hs, flow, runoff, mat, matt, keep, below, held, moved, ds):
    local_part(depth, hs, flow, runoff, mat, matt, keep, below, held, moved, ds)


def edges_now(flags2, ekeep, eflow, mine, gots, store):
    even, chip_even = flags2
    g0, g1, g2, g3 = gots
    choice = ((even, g0, g1), (chip_even, g2, g3), (even, g1, g0), (chip_even, g3, g2))
    for k, (flag, a, b) in enumerate(choice):
        for at in range(0, B, L):
            r = slice(at, at + L)
            e = slice(k * B + at, k * B + at + L)
            theirs = jnp.where(flag, a[r, :], b[r, :])
            ours = mine[e, :]
            up, low = (ours, theirs) if k < 2 else (theirs, ours)
            bed, below = ekeep[e, EUP : EUP + 1], ekeep[e, EDN : EDN + 1]
            q = momentum(
                eflow[e, :],
                up,
                bed + up,
                below + low,
                jnp.maximum(bed, below),
                ekeep[e, E1 : E1 + 1],
                ekeep[e, E2 : E2 + 1],
                ekeep[e, E3 : E3 + 1],
            )
            net = q * ekeep[e, EW : EW + 1]
            store(k, e, q, -net if k < 2 else net)


def begin_edges(flags2, ekeep, ekeep_in, eflow, flow_s, gots):
    even, chip_even = flags2
    g0, g1, g2, g3 = gots
    ekeep[...] = ekeep_in[...]
    eflow[0:H, :] = flow_s[...]
    for k, (flag, a, b) in enumerate(((even, g0, g1), (chip_even, g2, g3))):
        told = jnp.where(flag, a[H : H + 8, :], b[H : H + 8, :])
        spread = jnp.concatenate(
            [jnp.broadcast_to(told[0:1, :], (8, L)), jnp.broadcast_to(told[1:2, :], (8, L))],
            axis=1,
        ).T
        ekeep[k * B : (k + 1) * B, EDN : EDN + 1] = spread[:, 0:1]
        eflow[H + k * B : H + (k + 1) * B, :] = jnp.where(flag, b[B:H, :], a[B:H, :])


def main_body(first, dev, held, es, er, ets, etr, ekeep_in, eflow, keep, mine, g0, g1, g2, g3, depth, hs, next_flow, sent, o0, o1, o2, o3, *rest):
    even, chip_even = flags(dev[0])
    gots = (g0, g1, g2, g3)
    if first:
        ekeep, ds, flow_now = rest
        begin_edges((even, chip_even), ekeep, ekeep_in, flow_now, eflow, gots)
        eflow = flow_now
    else:
        ekeep = ekeep_in
        (ds,) = rest

    def store(k, e, q, net):
        next_flow[e, :] = q
        put_split(ds, e, net)

    edges_now((even, chip_even), ekeep, eflow, mine, gots, store)
    for a, b in ((0, H), (H, N)):
        r = slice(a, b)
        got = joined(dot(ets[r, :], ds[0:H, :]) + dot(etr[r, :], ds[H:N, :]))
        h = held[r, :] + keep[r, C4 : C4 + 1] * got
        depth[r, :] = h
        put_split(hs, r, h)
    sent[0:H, :] = joined(dot(es[...], hs[...]))
    sent[H:N, :] = joined(dot(er[...], hs[...]))
    route(
        even, chip_even, (o0, o1, o2, o3),
        sent[0:B, :], sent[B:H, :], sent[H : H + B, :], sent[H + B : N, :],
    )


def last_flow_body(dev, ets, ekeep, eflow, keep, moved, mine, g0, g1, g2, g3, ds, out_flow, sums, qs):
    def store(k, e, q, net):
        put_split(ds, e, net)
        if k < 2:
            put_split(qs, e, q)

    edges_now(flags(dev[0]), ekeep, eflow, mine, (g0, g1, g2, g3), store)
    for a, b in ((0, H), (H, N)):
        r = slice(a, b)
        got = joined(dot(ets[r, :], qs[...]))
        q = jnp.where(keep[r, REM : REM + 1] > 0.0, got, moved[r, :])
        out_flow[r, :] = q
        for k in range(a // L, b // L):
            part = q[k * L - a : (k + 1) * L - a, :].T
            sums[k : k + 1, :] = jnp.sum(part, axis=0, keepdims=True)


def last_depth_body(held, ets, etr, keep, ds, depth):
    for a, b in ((0, H), (H, N)):
        r = slice(a, b)
        got = joined(dot(ets[r, :], ds[0:H, :]) + dot(etr[r, :], ds[H:N, :]))
        depth[r, :] = held[r, :] + keep[r, C4 : C4 + 1] * got


def routes(n):
    on = [(i, i ^ 1) for i in range(n)]
    cross = [(i, (((i - 1) % n) ^ 1) + 1) for i in range(n)]
    cross = [(i, j % n) for i, j in cross]
    near = [(i, i ^ 2) for i in range(n)]
    far = [(i, ((((i - 2) % n) ^ 2) + 2) % n) for i in range(n)]
    return on, cross, near, far


def exchange(parts, n):
    on, cross, near, far = routes(n)
    g3 = lax.ppermute(parts[3], "basin", far)
    g1 = lax.ppermute(parts[1], "basin", cross)
    g2 = lax.ppermute(parts[2], "basin", near)
    g0 = lax.ppermute(parts[0], "basin", on)
    return g0, g1, g2, g3


def per_device(downstream, bed_level, reach_length, channel_width, roughness, depth, flow, runoff):
    n = lax.axis_size("basin")
    dev = lax.axis_index("basin").astype(jnp.int32).reshape(1)
    facts = jnp.zeros((5, 8, L), F32)
    for k, x in enumerate((downstream.astype(F32), bed_level, reach_length, channel_width, roughness)):
        facts = facts + jnp.pad(x.reshape(1, 8, L), ((k, 4 - k), (0, 0), (0, 0)))
    wide, split = ((N, L), F32), ((N, 2 * L), BF16)
    narrow = ((N, 8), F32)
    half, tall, full = ((H, N), BF16), ((N, H), BF16), ((N, N), BF16)
    vm = lambda st: pltpu.VMEM(*st)
    work = 4 * N * N * 512
    rows, cols, ets, note1, note2 = call(
        first_body,
        [((16, N), F32), ((N, 16), F32), tall, ((16, L), F32), ((16, L), F32)],
        [],
        work,
        [dev, facts],
        "sv",
    )
    got = exchange((note1, note1, note2, note2), n)
    es, mat, below, mine_s, flow_s, hs = call(
        leaving_body,
        [half, full, narrow, ((H, L), F32), ((H, L), F32), split],
        [vm(split)],
        work,
        [rows, cols, depth, flow],
        "v" * 4,
    )
    er, etr, ekeep, mine, *sent = call(
        entering_body,
        [half, tall, narrow, wide] + [((H + 8, L), F32)] * 4,
        [],
        work,
        [dev, rows, note1, note2, *got, hs, mine_s, flow_s],
        "s" + "v" * 10,
    )
    eflow = flow_s
    for step in range(STEPS):
        got = exchange(sent, n)
        if step == 0:
            matt, held, moved = call(
                start_body,
                [full, wide, wide],
                [vm(split)],
                work,
                [rows, cols, depth, hs, flow, runoff, mat, below],
                "v" * 8,
            )
        else:
            held, moved = call(
                local_body,
                [wide, wide],
                [vm(split)],
                work,
                [depth, hs, moved, runoff, mat, matt, cols, below],
                "v" * 8,
            )
        if step == STEPS - 1:
            ds, out_flow, sums = call(
                last_flow_body,
                [split, wide, ((8, L), F32)],
                [pltpu.VMEM((H, 2 * L), BF16)],
                work,
                [dev, ets, ekeep, eflow, cols, moved, mine, *got],
                "s" + "v" * 10,
            )
        else:
            first = step == 0
            depth, hs, eflow, mine, *sent = call(
                functools.partial(main_body, first),
                [wide, split, wide, wide] + [((B, L), F32)] * 4 + ([narrow] if first else []),
                [vm(split)] + ([vm(wide)] if first else []),
                work,
                [dev, held, es, er, ets, etr, ekeep, eflow, cols, mine, *got],
                "s" + "v" * 13,
            )
            if first:
                ekeep = sent.pop()
    m = lax.axis_size("ens")
    parts = [lax.ppermute(sums, "ens", [(i, i ^ k) for i in range(m)]) for k in range(1, m)]
    (depth,) = call(last_depth_body, [wide], [], work, [held, ets, etr, cols, ds], "v" * 5)
    if m == 4:
        total = (sums + parts[0]) + (parts[1] + parts[2])
    else:
        total = sums + parts[0]
    return depth, out_flow, (total / (m * depth.shape[1])).reshape(N)


def solution(mesh):
    placed = (
        P("basin"),
        P("basin"),
        P("basin"),
        P("basin"),
        P("basin"),
        P("basin", "ens"),
        P("basin", "ens"),
        P("basin", "ens"),
    )
    return jax.shard_map(
        per_device,
        mesh=mesh,
        in_specs=placed,
        out_specs=(P("basin", "ens"), P("basin", "ens"), P("basin")),
        check_vma=False,
    )
```
